256 devices in a mesh: shard: 64 (over x, z, core), rep: 4 (over y).
Axes of the slice: x: 4, y: 4, z: 8, core: 2. Of those that a mesh axis runs over, the one named last changes fastest.
Arguments:
- entities: bfloat16 [98304, 400], P(('shard', 'rep')), may hold values from -6 to 6
- row_state: float32 [98304], P(('shard', 'rep')), may hold values from 0.01 to 1
- relations: bfloat16 [512, 400], replicated, may hold values from -0.59765625 to 0.59765625
- requests: int32 [16384, 48], P(('shard', 'rep')), may hold values from -1 to 1535, as said below
- head_slots: int32 [768, 512], P(('shard', 'rep')), may hold values from 0 to 3071, as said below
- tail_slots: int32 [768, 512], P(('shard', 'rep')), may hold values from 0 to 3071, as said below
- neg_slots: int32 [768, 512], P(('shard', 'rep')), may hold values from 0 to 3071, as said below
- relation_ids: int32 [256, 3], P(('shard', 'rep')), may hold values from 0 to 511
Outputs:
- new_entities: bfloat16 [98304, 400], P(('shard', 'rep'))
- new_state: float32 [98304], P(('shard', 'rep'))
The draws below stay inside these ranges and needn't reach their ends.
Inputs may be any that keep to these rules, and one draw needn't show every extreme that they name: `requests`: row r is device r // 64's list for peer r % 64 along shard: ids among that peer's 4 * 384 entity rows, or -1 for an empty entry. Live entries come first and are distinct within a list; every list has one live entry or more; every device fills some list, and in every draw some peer's lists are full from every device. `head_slots`: each value p * 48 + c names a live entry of the same device's list for peer p. `tail_slots`: each value p * 48 + c names a live entry of the same device's list for peer p. `neg_slots`: each value p * 48 + c names a live entry of the same device's list for peer p.
All inputs are finite; a program needn't handle non-finite values.
Results may differ from the reference program's by a relative error of at most 0.0035.
Values may be sent and summed in bfloat16 or wider, within the bound.
No kernel may reach another device: no remote copies, remote signals or barrier semaphores. Data moves between devices by JAX's collectives and lax.ppermute only.
A program may use at most 128 MiB of HBM per device.

```python
import math
import jax
import jax.numpy as jnp
from jax import lax

D = 400
ENT_DEV = 384
CAP = 48
BLOCKS = 3
EDGE = 512
NEG = 512
REL = 512
ENTITIES = 98304
N_SHARD = 64
N_REP = 4


def list_counts(key):
    devices = N_SHARD * N_REP
    keys = jax.random.split(jax.random.fold_in(key, 7), 4)
    weights = jax.random.randint(keys[0], (N_SHARD,), 1, 5)
    base = jax.random.randint(keys[1], (devices, N_SHARD), 1, CAP // 3 + 1) * weights[None, :]
    starred = jax.random.randint(keys[2], (devices, 1), 0, N_SHARD)
    full_peer = jax.random.randint(keys[3], (), 0, N_SHARD)
    peer_ids = jnp.arange(N_SHARD)[None, :]
    return jnp.where((peer_ids == starred) | (peer_ids == full_peer), CAP, jnp.minimum(base, CAP)).astype(jnp.int32)


def slot_draw(key, width, salt):
    devices = N_SHARD * N_REP
    counts = list_counts(key)
    keys = jax.random.split(jax.random.fold_in(key, salt), 2)
    peers = jax.random.randint(keys[0], (devices, BLOCKS * width), 0, N_SHARD)
    limits = jnp.take_along_axis(counts, peers, axis=1)
    entries = jax.random.randint(keys[1], (devices, BLOCKS * width), 0, limits)
    return (peers * CAP + entries).reshape(devices * BLOCKS, width).astype(jnp.int32)


def draw_requests(key, part):
    devices = N_SHARD * N_REP
    counts = list_counts(key)
    keys = jax.random.split(jax.random.fold_in(key, 11), 2)
    stride = N_REP * ENT_DEV // CAP
    shifts = jax.random.randint(keys[0], (devices, N_SHARD, 1), 0, CAP)
    jitter = jax.random.randint(keys[1], (devices, N_SHARD, CAP), 0, stride)
    entry = jnp.arange(CAP)[None, None, :]
    ids = (entry + shifts) % CAP * stride + jitter
    ids = jnp.where(entry < counts[:, :, None], ids, -1)
    return ids.reshape(devices * N_SHARD, CAP).astype(jnp.int32)


def draw_head_slots(key, part):
    return slot_draw(key, EDGE, 21)


def draw_tail_slots(key, part):
    return slot_draw(key, EDGE, 22)


def draw_neg_slots(key, part):
    return slot_draw(key, NEG, 23)


def plant(drawn, key, smallest, top_value):
    index_at = [jax.random.randint(jax.random.fold_in(key, axis), (), 0, length) for axis, length in enumerate(drawn.shape)]
    widest = drawn.shape.index(max(drawn.shape))
    next_to = index_at[:widest] + [(index_at[widest] + 1) % drawn.shape[widest]] + index_at[widest + 1:]
    return drawn.at[tuple(index_at)].set(smallest).at[tuple(next_to)].set(top_value)


def shard_levels(stream_key, dims, cuts, smallest, high):
    level, own = 1.0, jax.random.fold_in(stream_key, 6)
    for dim, parts in cuts:
        steps = jnp.exp(jax.random.uniform(jax.random.fold_in(own, dim), (parts,), jnp.float32, smallest / len(cuts), high / len(cuts)))
        level = level * jnp.repeat(steps, dims[dim] // parts).reshape([-1 if axis == dim else 1 for axis in range(len(dims))])
    return level


def noise(stream_key, shape, scale, reach, cuts=(), kind=jnp.bfloat16):
    factor_of = shard_levels(stream_key, shape, cuts, -0.22, 0.18) if cuts else 1.0
    drawn = jax.random.normal(stream_key, shape, jnp.float32) * scale * factor_of
    return jnp.minimum(jnp.maximum(drawn, -reach), reach).astype(kind)


def setup_inputs(seed: int = 0) -> dict:
    key_list = jax.random.split(jax.random.key(seed), 9)
    entities = noise(key_list[0], (ENTITIES, D), 1.0, 6.0, ((0, 256),))
    row_state = jnp.clip(jnp.exp(math.log(1.0) - 4.6051702 * jax.random.uniform(key_list[1], (ENTITIES,), jnp.float32) ** shard_levels(key_list[1], (ENTITIES,), ((0, 256),), -0.2, 0.2)), 0.01, 1.0)
    relations = noise(key_list[2], (REL, D), 0.1, 0.59765625)
    requests = draw_requests(jax.random.fold_in(key_list[8], 71), 0)
    head_slots = draw_head_slots(jax.random.fold_in(key_list[8], 71), 0)
    tail_slots = draw_tail_slots(jax.random.fold_in(key_list[8], 71), 0)
    neg_slots = draw_neg_slots(jax.random.fold_in(key_list[8], 71), 0)
    relation_ids = plant(jax.random.randint(key_list[7], (N_SHARD * N_REP, BLOCKS), 0, REL), jax.random.fold_in(key_list[7], 1), 0, REL - 1).astype(jnp.int32)
    return {"entities": entities, "row_state": row_state, "relations": relations, "requests": requests, "head_slots": head_slots, "tail_slots": tail_slots, "neg_slots": neg_slots, "relation_ids": relation_ids}


learning_rate = 0.1

def span_free_grads(head_rows, tail_rows, neg_rows, relation):
    half_width = head_rows.shape[1] // 2
    head_real = head_rows[:, :half_width].astype(jnp.float32)
    head_imag = head_rows[:, half_width:].astype(jnp.float32)
    tail_real = tail_rows[:, :half_width].astype(jnp.float32)
    tail_imag = tail_rows[:, half_width:].astype(jnp.float32)
    rel_real = relation[:half_width].astype(jnp.float32)
    rel_imag = relation[half_width:].astype(jnp.float32)
    queries = jnp.concatenate([head_real * rel_real - head_imag * rel_imag, head_real * rel_imag + head_imag * rel_real], axis=1)
    probes = jnp.concatenate([rel_real * tail_real + rel_imag * tail_imag, rel_real * tail_imag - rel_imag * tail_real], axis=1)
    positives = lax.optimization_barrier(jnp.sum(queries * tail_rows.astype(jnp.float32), axis=1))
    queries_low = queries.astype(jnp.bfloat16)
    probes_low = probes.astype(jnp.bfloat16)
    contract_last = (((1,), (1,)), ((), ()))
    contract_first = (((0,), (0,)), ((), ()))
    tail_scores = lax.dot_general(queries_low, neg_rows, contract_last, preferred_element_type=jnp.float32)
    head_scores = lax.dot_general(probes_low, neg_rows, contract_last, preferred_element_type=jnp.float32)
    neg_total = neg_rows.shape[0]
    positive_grad = -jax.nn.sigmoid(-positives)
    tail_weights = (jax.nn.sigmoid(tail_scores) / neg_total).astype(jnp.bfloat16)
    head_weights = (jax.nn.sigmoid(head_scores) / neg_total).astype(jnp.bfloat16)
    dquery = positive_grad[:, None] * tail_rows.astype(jnp.float32) + jnp.dot(tail_weights, neg_rows, preferred_element_type=jnp.float32)
    dprobe = jnp.dot(head_weights, neg_rows, preferred_element_type=jnp.float32)
    neg_grad = lax.dot_general(tail_weights, queries_low, contract_first, preferred_element_type=jnp.float32)
    neg_grad = neg_grad + lax.dot_general(head_weights, probes_low, contract_first, preferred_element_type=jnp.float32)
    dquery_real = dquery[:, :half_width]
    dquery_imag = dquery[:, half_width:]
    dprobe_real = dprobe[:, :half_width]
    dprobe_imag = dprobe[:, half_width:]
    head_grad = jnp.concatenate([dquery_real * rel_real + dquery_imag * rel_imag, dquery_imag * rel_real - dquery_real * rel_imag], axis=1)
    tail_grad = positive_grad[:, None] * queries + jnp.concatenate([dprobe_real * rel_real - dprobe_imag * rel_imag, dprobe_real * rel_imag + dprobe_imag * rel_real], axis=1)
    return (head_grad, tail_grad, neg_grad)

def reference(entities, row_state, relations, requests, head_slots, tail_slots, neg_slots, relation_ids):
    devices = N_SHARD * N_REP
    slab_len = N_REP * ENT_DEV
    total_rows = entities.shape[0]
    row_width = entities.shape[1]
    owners = (jnp.arange(N_SHARD).astype(jnp.int32) * slab_len)[:, None]

    def one_device(grad_sum, inputs):
        wanted, head_ids, tail_ids, neg_ids, rel_row = inputs
        live_mask = wanted >= 0
        global_ids = (owners + jnp.maximum(wanted, 0)).astype(jnp.int32)
        fetched = jnp.where(live_mask[..., None], entities[global_ids], jnp.zeros((), entities.dtype)).reshape(-1, row_width)
        slot_grads = jnp.zeros((fetched.shape[0], row_width), jnp.float32)
        for block_index in range(BLOCKS):
            head_grad, tail_grad, neg_grad = span_free_grads(fetched[head_ids[block_index]], fetched[tail_ids[block_index]], fetched[neg_ids[block_index]], relations[rel_row[block_index]])
            slot_grads = slot_grads.at[head_ids[block_index]].add(head_grad)
            slot_grads = slot_grads.at[tail_ids[block_index]].add(tail_grad)
            slot_grads = slot_grads.at[neg_ids[block_index]].add(neg_grad)
        targets = jnp.where(live_mask, global_ids, total_rows).reshape(-1).astype(jnp.int32)
        grad_sum = grad_sum.at[targets].add(slot_grads, mode='drop')
        return (grad_sum, None)
    scanned = (requests.reshape(devices, N_SHARD, CAP), head_slots.reshape(devices, BLOCKS, EDGE), tail_slots.reshape(devices, BLOCKS, EDGE), neg_slots.reshape(devices, BLOCKS, NEG), relation_ids)
    entity_grads, _ = lax.scan(one_device, jnp.zeros((total_rows, row_width), jnp.float32), scanned)
    new_state = row_state + lax.optimization_barrier(jnp.mean(entity_grads * entity_grads, axis=1))
    new_entities = (entities.astype(jnp.float32) - learning_rate * entity_grads / jnp.sqrt(new_state)[:, None]).astype(jnp.bfloat16)
    return (new_entities, new_state)
```

```python
import jax
import jax.numpy as jnp
from jax import lax
from jax.experimental import pallas as pl
from jax.experimental.pallas import tpu as pltpu
from jax.sharding import PartitionSpec as P

learning_rate = 0.1
LANES = 128
SPLIT = 256
WIDE = 2 * SPLIT
TILES = WIDE // LANES
VMEM_LIMIT = 60 * 1024 * 1024


def spread(rows):
    half = rows.shape[1] // 2
    pad = ((0, 0), (0, SPLIT - half))
    return jnp.concatenate([jnp.pad(rows[:, :half], pad), jnp.pad(rows[:, half:], pad)], axis=1)


def serve_kernel(wanted_ref, slab_ref, out_ref):
    peers, cap = wanted_ref.shape
    slab_len = slab_ref.shape[0]
    columns = wanted_ref[...].T
    iota = lax.broadcasted_iota(jnp.int32, (cap, slab_len), 1)
    picks = [
        jnp.where(columns[:, p : p + 1] == iota, 1.0, 0.0).astype(jnp.bfloat16) for p in range(peers)
    ]
    picked = jnp.concatenate(picks, axis=0)
    rows = jnp.dot(picked, slab_ref[...], preferred_element_type=jnp.float32)
    out_ref[...] = rows.astype(jnp.bfloat16).reshape(out_ref.shape)


def serve(wanted, slab):
    peers, cap = wanted.shape
    step = 8
    return pl.pallas_call(
        serve_kernel,
        grid=(peers // step,),
        in_specs=[
            pl.BlockSpec((step, cap), lambda i: (i, 0)),
            pl.BlockSpec(slab.shape, lambda i: (0, 0)),
        ],
        out_specs=pl.BlockSpec((step, cap, WIDE), lambda i: (i, 0, 0)),
        out_shape=jax.ShapeDtypeStruct((peers, cap, WIDE), jnp.bfloat16),
        compiler_params=pltpu.CompilerParams(vmem_limit_bytes=VMEM_LIMIT),
        name="serve",
    )(wanted, slab)


def collect_kernel(wanted_ref, rows_ref, out_ref):
    step = out_ref.shape[0]
    groups, lanes = wanted_ref.shape
    base = pl.program_id(0) * step
    iota = lax.broadcasted_iota(jnp.int32, (step, lanes), 0) + base
    picks = [
        jnp.where(wanted_ref[g : g + 1, :] == iota, 1.0, 0.0).astype(jnp.bfloat16) for g in range(groups)
    ]
    picked = jnp.concatenate(picks, axis=1)
    out_ref[...] = jnp.dot(picked, rows_ref[...], preferred_element_type=jnp.float32).astype(out_ref.dtype)


def collect(wanted, rows, slab_len):
    step = 256
    return pl.pallas_call(
        collect_kernel,
        grid=(slab_len // step,),
        in_specs=[
            pl.BlockSpec(wanted.shape, lambda i: (0, 0)),
            pl.BlockSpec(rows.shape, lambda i: (0, 0)),
        ],
        out_specs=pl.BlockSpec((step, WIDE), lambda i: (i, 0)),
        out_shape=jax.ShapeDtypeStruct((slab_len, WIDE), jnp.bfloat16),
        compiler_params=pltpu.CompilerParams(vmem_limit_bytes=VMEM_LIMIT),
        name="collect",
    )(wanted, rows)


def interleaved(ref, start, count):
    return [ref[pl.ds(start * TILES + k, count, stride=TILES), :] for k in range(TILES)]


def put_interleaved(ref, start, count, tiles):
    for k in range(TILES):
        ref[pl.ds(start * TILES + k, count, stride=TILES), :] = tiles[k]


def pair(tiles):
    return jnp.concatenate(tiles[:2], axis=1), jnp.concatenate(tiles[2:], axis=1)


def unpair(real, imag):
    return [real[:, :LANES], real[:, LANES:], imag[:, :LANES], imag[:, LANES:]]


def edge_kernel(
    head_ids, tail_ids, neg_ids, rel_ref, fetched_ref, out_ref,
    source, heads, tails, negs, sum_a, sum_b, sum_c, negs_low, pairs_low, weights_low,
):
    slots = fetched_ref.shape[0]
    blocks, edges = head_ids.shape
    chunk = 256

    @pl.loop(0, slots // chunk)
    def _(c):
        start = c * chunk
        block = fetched_ref[pl.ds(pl.multiple_of(start, chunk), chunk), :].astype(jnp.float32)
        put_interleaved(source, start, chunk, [block[:, k * LANES : (k + 1) * LANES] for k in range(TILES)])
        zeros = jnp.zeros((chunk * TILES, LANES), jnp.float32)
        for total in (sum_a, sum_b, sum_c):
            total[pl.ds(pl.multiple_of(start * TILES, chunk * TILES), chunk * TILES), :] = zeros

    @pl.loop(0, blocks)
    def _(b):
        unroll = 16

        @pl.loop(0, edges // unroll)
        def _(step):
            for u in range(unroll):
                j = step * unroll + u
                for ids, rows in ((head_ids, heads), (tail_ids, tails), (neg_ids, negs)):
                    at = pl.multiple_of(ids[b, j] * TILES, TILES)
                    rows[pl.ds(pl.multiple_of(j * TILES, TILES), TILES), :] = source[pl.ds(at, TILES), :]

        negs_low[...] = jnp.concatenate(
            [tile.astype(jnp.bfloat16) for tile in interleaved(negs, 0, edges)], axis=1
        )
        rel_re = rel_ref[pl.ds(b, 1), :SPLIT]
        rel_im = rel_ref[pl.ds(b, 1), SPLIT:]
        for c in range(edges // chunk):
            start = c * chunk
            head_re, head_im = pair(interleaved(heads, start, chunk))
            tail_re, tail_im = pair(interleaved(tails, start, chunk))
            query_re = head_re * rel_re - head_im * rel_im
            query_im = head_re * rel_im + head_im * rel_re
            probe_re = rel_re * tail_re + rel_im * tail_im
            probe_im = rel_re * tail_im - rel_im * tail_re
            positives = jnp.sum(query_re * tail_re + query_im * tail_im, axis=1, keepdims=True)
            positive_grad = -jax.nn.sigmoid(-positives)
            queries_low = jnp.concatenate([query_re, query_im], axis=1).astype(jnp.bfloat16)
            probes_low = jnp.concatenate([probe_re, probe_im], axis=1).astype(jnp.bfloat16)
            both = jnp.concatenate([queries_low, probes_low], axis=0)
            pairs_low[2 * start : 2 * start + 2 * chunk, :] = both
            scores = lax.dot_general(
                both, negs_low[...], (((1,), (1,)), ((), ())), preferred_element_type=jnp.float32
            )
            scale = 0.5 / edges
            weights = (jnp.tanh(scores * 0.5) * scale + scale).astype(jnp.bfloat16)
            weights_low[2 * start : 2 * start + 2 * chunk, :] = weights
            grads = jnp.dot(weights, negs_low[...], preferred_element_type=jnp.float32)
            dquery_re = positive_grad * tail_re + grads[:chunk, :SPLIT]
            dquery_im = positive_grad * tail_im + grads[:chunk, SPLIT:]
            dprobe_re = grads[chunk:, :SPLIT]
            dprobe_im = grads[chunk:, SPLIT:]
            put_interleaved(
                heads, start, chunk,
                unpair(dquery_re * rel_re + dquery_im * rel_im, dquery_im * rel_re - dquery_re * rel_im),
            )
            put_interleaved(
                tails, start, chunk,
                unpair(
                    positive_grad * query_re + dprobe_re * rel_re - dprobe_im * rel_im,
                    positive_grad * query_im + dprobe_re * rel_im + dprobe_im * rel_re,
                ),
            )
        neg_grad = lax.dot_general(
            weights_low[...], pairs_low[...], (((0,), (0,)), ((), ())), preferred_element_type=jnp.float32
        )
        put_interleaved(negs, 0, edges, [neg_grad[:, k * LANES : (k + 1) * LANES] for k in range(TILES)])

        @pl.loop(0, edges // unroll)
        def _(step):
            for u in range(unroll):
                j = step * unroll + u
                for ids, rows, total in (
                    (head_ids, heads, sum_a), (tail_ids, tails, sum_b), (neg_ids, negs, sum_c)
                ):
                    at = pl.multiple_of(ids[b, j] * TILES, TILES)
                    total[pl.ds(at, TILES), :] += rows[pl.ds(pl.multiple_of(j * TILES, TILES), TILES), :]

    @pl.loop(0, slots // chunk)
    def _(c):
        start = c * chunk
        parts = [interleaved(total, start, chunk) for total in (sum_a, sum_b, sum_c)]
        out_ref[pl.ds(pl.multiple_of(start, chunk), chunk), :] = jnp.concatenate(
            [(x + y + z).astype(jnp.bfloat16) for x, y, z in zip(*parts)], axis=1
        )


def edge_grads(head_ids, tail_ids, neg_ids, rel, fetched):
    slots = fetched.shape[0]
    edges = head_ids.shape[1]
    smem = pl.BlockSpec(memory_space=pltpu.SMEM)
    vmem = pl.BlockSpec(memory_space=pltpu.VMEM)
    rows = pltpu.VMEM((edges * TILES, LANES), jnp.float32)
    total = pltpu.VMEM((slots * TILES, LANES), jnp.float32)
    return pl.pallas_call(
        edge_kernel,
        in_specs=[smem, smem, smem, vmem, vmem],
        out_specs=vmem,
        out_shape=jax.ShapeDtypeStruct((slots, WIDE), jnp.bfloat16),
        scratch_shapes=[
            total, rows, rows, rows, total, total, total,
            pltpu.VMEM((edges, WIDE), jnp.bfloat16),
            pltpu.VMEM((2 * edges, WIDE), jnp.bfloat16),
            pltpu.VMEM((2 * edges, edges), jnp.bfloat16),
        ],
        compiler_params=pltpu.CompilerParams(vmem_limit_bytes=VMEM_LIMIT),
        name="edges",
    )(head_ids, tail_ids, neg_ids, rel, fetched)


def local(
    entities, row_state, relations, requests, head_slots, tail_slots, neg_slots, relation_ids
):
    own_rows, row_width = entities.shape
    half = row_width // 2
    peer_count, slot_cap = requests.shape
    slots = peer_count * slot_cap
    wanted = lax.all_to_all(requests, "shard", split_axis=0, concat_axis=0, tiled=True)
    slab = lax.all_gather(spread(entities), "rep", axis=0, tiled=True)
    served = serve(wanted, slab)
    fetched = lax.all_to_all(served, "shard", split_axis=0, concat_axis=0, tiled=True)
    rel = spread(relations[relation_ids[0]].astype(jnp.float32))
    slot_grads = edge_grads(head_slots, tail_slots, neg_slots, rel, fetched.reshape(slots, WIDE))
    returned = lax.all_to_all(
        slot_grads.reshape(peer_count, slot_cap, WIDE), "shard", split_axis=0, concat_axis=0, tiled=True
    )
    slab_len = slab.shape[0]
    slab_grads = collect(wanted.reshape(slots // LANES, LANES), returned.reshape(slots, WIDE), slab_len)
    row_grads = lax.psum_scatter(slab_grads, "rep", scatter_dimension=0, tiled=True).astype(jnp.float32)
    row_grads = jnp.concatenate([row_grads[:, :half], row_grads[:, SPLIT : SPLIT + half]], axis=1)
    new_state = row_state + jnp.mean(row_grads * row_grads, axis=1)
    new_entities = (
        entities.astype(jnp.float32) - learning_rate * row_grads / jnp.sqrt(new_state)[:, None]
    ).astype(jnp.bfloat16)
    return (new_entities, new_state)


def solution(mesh):
    placed = (
        P(("shard", "rep"), None),
        P(("shard", "rep")),
        P(),
        P(("shard", "rep"), None),
        P(("shard", "rep"), None),
        P(("shard", "rep"), None),
        P(("shard", "rep"), None),
        P(("shard", "rep"), None),
    )
    return jax.shard_map(
        local,
        mesh=mesh,
        in_specs=placed,
        out_specs=(P(("shard", "rep"), None), P(("shard", "rep"))),
        check_vma=False,
    )
```

```python
import jax
import jax.numpy as jnp
from jax import lax
from jax.experimental import pallas as pl
from jax.experimental.pallas import tpu as pltpu
from jax.sharding import PartitionSpec as P

learning_rate = 0.1
LANES = 128
SPLIT = 256
WIDE = 2 * SPLIT
TILES = WIDE // LANES
VMEM_LIMIT = 60 * 1024 * 1024


WIRE = 160
GROUP = 16
TAIL = 16


def spread(rows):
    half = rows.shape[1] // 2
    pad = ((0, 0), (0, SPLIT - half))
    return jnp.concatenate([jnp.pad(rows[:, :half], pad), jnp.pad(rows[:, half:], pad)], axis=1)


def wire_order(rows):
    half = rows.shape[1] // 2
    filler = jnp.zeros((rows.shape[0], WIDE - 2 * half), rows.dtype)
    return jnp.concatenate(
        [rows[:, :LANES], rows[:, half : half + LANES], rows[:, LANES:half], rows[:, half + LANES :], filler],
        axis=1,
    )


def row_order(rows):
    real = jnp.concatenate([rows[:, :LANES], rows[:, 256:328]], axis=1)
    imag = jnp.concatenate([rows[:, LANES:256], rows[:, 328:400]], axis=1)
    return jnp.concatenate([real, imag], axis=1)


def serve_kernel(wanted_ref, slab_ref, out_ref):
    peers, cap = wanted_ref.shape
    slab_len = slab_ref.shape[0]
    columns = wanted_ref[...].T
    iota = lax.broadcasted_iota(jnp.int32, (cap, slab_len), 1)
    picks = [
        jnp.where(columns[:, p : p + 1] == iota, 1.0, 0.0).astype(jnp.bfloat16) for p in range(peers)
    ]
    picked = jnp.concatenate(picks, axis=0)
    rows = jnp.dot(picked, slab_ref[...], preferred_element_type=jnp.float32)
    for k in range(3):
        tile = rows[:, k * LANES : (k + 1) * LANES].astype(jnp.bfloat16).reshape(peers, cap, LANES)
        out_ref[:, k * cap : (k + 1) * cap, :] = tile
    tail = rows[:, 3 * LANES :].reshape(peers, cap // GROUP, GROUP, LANES)
    packed = tail[:, 0]
    for g in range(1, cap // GROUP):
        packed = packed + pltpu.roll(tail[:, g], g * TAIL, axis=2)
    out_ref[:, 3 * cap :, :] = packed.astype(jnp.bfloat16)


def serve(wanted, slab):
    peers, cap = wanted.shape
    step = 8
    return pl.pallas_call(
        serve_kernel,
        grid=(peers // step,),
        in_specs=[
            pl.BlockSpec((step, cap), lambda i: (i, 0)),
            pl.BlockSpec(slab.shape, lambda i: (0, 0)),
        ],
        out_specs=pl.BlockSpec((step, WIRE, LANES), lambda i: (i, 0, 0)),
        out_shape=jax.ShapeDtypeStruct((peers, WIRE, LANES), jnp.bfloat16),
        compiler_params=pltpu.CompilerParams(vmem_limit_bytes=VMEM_LIMIT),
        name="serve",
    )(wanted, slab)


def collect_kernel(wanted_ref, rows_ref, out_ref, rows_wide):
    step = out_ref.shape[0]
    groups, lanes = wanted_ref.shape
    peers = rows_ref.shape[0]
    cap = (WIRE - GROUP) // 3
    base = pl.program_id(0) * step

    @pl.when(pl.program_id(0) == 0)
    def _():
        for k in range(3):
            tile = rows_ref[:, k * cap : (k + 1) * cap, :]
            rows_wide[:, k * LANES : (k + 1) * LANES] = tile.reshape(peers * cap, LANES)
        packed = rows_ref[:, 3 * cap :, :].astype(jnp.float32)
        lane = lax.broadcasted_iota(jnp.int32, packed.shape, 2)
        tails = [
            jnp.where((lane >= g * TAIL) & (lane < (g + 1) * TAIL), packed, 0.0).astype(jnp.bfloat16)
            for g in range(cap // GROUP)
        ]
        rows_wide[:, 3 * LANES :] = jnp.concatenate(tails, axis=1).reshape(peers * cap, LANES)

    iota = lax.broadcasted_iota(jnp.int32, (step, lanes), 0) + base
    picks = [
        jnp.where(wanted_ref[g : g + 1, :] == iota, 1.0, 0.0).astype(jnp.bfloat16) for g in range(groups)
    ]
    picked = jnp.concatenate(picks, axis=1)
    sums = jnp.dot(picked, rows_wide[...], preferred_element_type=jnp.float32)
    tail = sums[:, 3 * LANES :]
    tail = tail + pltpu.roll(tail, LANES - TAIL, axis=1) + pltpu.roll(tail, LANES - 2 * TAIL, axis=1)
    lane = lax.broadcasted_iota(jnp.int32, tail.shape, 1)
    tail = jnp.where(lane < TAIL, tail, 0.0)
    out_ref[...] = jnp.concatenate([sums[:, : 3 * LANES], tail], axis=1).astype(out_ref.dtype)


def collect(wanted, rows, slab_len):
    step = 256
    slots = wanted.shape[0] * wanted.shape[1]
    return pl.pallas_call(
        collect_kernel,
        grid=(slab_len // step,),
        in_specs=[
            pl.BlockSpec(wanted.shape, lambda i: (0, 0)),
            pl.BlockSpec(rows.shape, lambda i: (0, 0, 0)),
        ],
        out_specs=pl.BlockSpec((step, WIDE), lambda i: (i, 0)),
        out_shape=jax.ShapeDtypeStruct((slab_len, WIDE), jnp.bfloat16),
        scratch_shapes=[pltpu.VMEM((slots, WIDE), jnp.bfloat16)],
        compiler_params=pltpu.CompilerParams(vmem_limit_bytes=VMEM_LIMIT),
        name="collect",
    )(wanted, rows)


def interleaved(ref, start, count):
    return [ref[pl.ds(start * TILES + k, count, stride=TILES), :] for k in range(TILES)]


def put_interleaved(ref, start, count, tiles):
    for k in range(TILES):
        ref[pl.ds(start * TILES + k, count, stride=TILES), :] = tiles[k]


def pair(tiles):
    return jnp.concatenate(tiles[:2], axis=1), jnp.concatenate(tiles[2:], axis=1)


def unpair(real, imag):
    return [real[:, :LANES], real[:, LANES:], imag[:, :LANES], imag[:, LANES:]]


def edge_kernel(
    head_ids, tail_ids, neg_ids, rel_ref, fetched_ref, out_ref,
    source, heads, tails, negs, sum_a, sum_b, sum_c, negs_low, pairs_low, weights_low,
):
    peers = fetched_ref.shape[0]
    cap = (WIRE - GROUP) // 3
    groups = cap // GROUP
    some = 8
    span = some * cap
    split = 72
    early = LANES - split
    blocks, edges = head_ids.shape
    chunk = 256

    @pl.loop(0, peers // some)
    def _(c):
        at = pl.ds(c * some, some)
        real, imag, tail = [
            fetched_ref[at, k * cap : (k + 1) * cap, :].astype(jnp.float32).reshape(span, LANES) for k in range(3)
        ]
        packed = fetched_ref[at, 3 * cap :, :].astype(jnp.float32)
        late = jnp.concatenate(
            [pltpu.roll(packed, early - g * TAIL, axis=2) for g in range(groups)], axis=1
        ).reshape(span, LANES)
        lane = lax.broadcasted_iota(jnp.int32, (span, LANES), 1)
        real_end = jnp.where(lane < split, tail, 0.0)
        imag_end = jnp.where(lane < early, pltpu.roll(tail, early, axis=1), jnp.where(lane < split, late, 0.0))
        put_interleaved(source, c * span, span, [real, real_end, imag, imag_end])
        zeros = jnp.zeros((span * TILES, LANES), jnp.float32)
        for total in (sum_a, sum_b, sum_c):
            total[pl.ds(pl.multiple_of(c * span * TILES, span * TILES), span * TILES), :] = zeros

    @pl.loop(0, blocks)
    def _(b):
        unroll = 16

        @pl.loop(0, edges // unroll)
        def _(step):
            for u in range(unroll):
                j = step * unroll + u
                for ids, rows in ((head_ids, heads), (tail_ids, tails), (neg_ids, negs)):
                    at = pl.multiple_of(ids[b, j] * TILES, TILES)
                    rows[pl.ds(pl.multiple_of(j * TILES, TILES), TILES), :] = source[pl.ds(at, TILES), :]

        negs_low[...] = jnp.concatenate(
            [tile.astype(jnp.bfloat16) for tile in interleaved(negs, 0, edges)], axis=1
        )
        rel_re = rel_ref[pl.ds(b, 1), :SPLIT]
        rel_im = rel_ref[pl.ds(b, 1), SPLIT:]
        for c in range(edges // chunk):
            start = c * chunk
            head_re, head_im = pair(interleaved(heads, start, chunk))
            tail_re, tail_im = pair(interleaved(tails, start, chunk))
            query_re = head_re * rel_re - head_im * rel_im
            query_im = head_re * rel_im + head_im * rel_re
            probe_re = rel_re * tail_re + rel_im * tail_im
            probe_im = rel_re * tail_im - rel_im * tail_re
            positives = jnp.sum(query_re * tail_re + query_im * tail_im, axis=1, keepdims=True)
            positive_grad = -jax.nn.sigmoid(-positives)
            queries_low = jnp.concatenate([query_re, query_im], axis=1).astype(jnp.bfloat16)
            probes_low = jnp.concatenate([probe_re, probe_im], axis=1).astype(jnp.bfloat16)
            both = jnp.concatenate([queries_low, probes_low], axis=0)
            pairs_low[2 * start : 2 * start + 2 * chunk, :] = both
            scores = lax.dot_general(
                both, negs_low[...], (((1,), (1,)), ((), ())), preferred_element_type=jnp.float32
            )
            scale = 0.5 / edges
            weights = (jnp.tanh(scores * 0.5) * scale + scale).astype(jnp.bfloat16)
            weights_low[2 * start : 2 * start + 2 * chunk, :] = weights
            grads = jnp.dot(weights, negs_low[...], preferred_element_type=jnp.float32)
            dquery_re = positive_grad * tail_re + grads[:chunk, :SPLIT]
            dquery_im = positive_grad * tail_im + grads[:chunk, SPLIT:]
            dprobe_re = grads[chunk:, :SPLIT]
            dprobe_im = grads[chunk:, SPLIT:]
            put_interleaved(
                heads, start, chunk,
                unpair(dquery_re * rel_re + dquery_im * rel_im, dquery_im * rel_re - dquery_re * rel_im),
            )
            put_interleaved(
                tails, start, chunk,
                unpair(
                    positive_grad * query_re + dprobe_re * rel_re - dprobe_im * rel_im,
                    positive_grad * query_im + dprobe_re * rel_im + dprobe_im * rel_re,
                ),
            )
        neg_grad = lax.dot_general(
            weights_low[...], pairs_low[...], (((0,), (0,)), ((), ())), preferred_element_type=jnp.float32
        )
        put_interleaved(negs, 0, edges, [neg_grad[:, k * LANES : (k + 1) * LANES] for k in range(TILES)])

        @pl.loop(0, edges // unroll)
        def _(step):
            for u in range(unroll):
                j = step * unroll + u
                for ids, rows, total in (
                    (head_ids, heads, sum_a), (tail_ids, tails, sum_b), (neg_ids, negs, sum_c)
                ):
                    at = pl.multiple_of(ids[b, j] * TILES, TILES)
                    total[pl.ds(at, TILES), :] += rows[pl.ds(pl.multiple_of(j * TILES, TILES), TILES), :]

    @pl.loop(0, peers // some)
    def _(c):
        at = pl.ds(c * some, some)
        parts = [interleaved(total, c * span, span) for total in (sum_a, sum_b, sum_c)]
        real, real_end, imag, imag_end = [x + y + z for x, y, z in zip(*parts)]
        lane = lax.broadcasted_iota(jnp.int32, (span, LANES), 1)
        tail = jnp.where(lane < split, real_end, pltpu.roll(imag_end, split, axis=1))
        for k, tile in enumerate((real, imag, tail)):
            out_ref[at, k * cap : (k + 1) * cap, :] = tile.astype(jnp.bfloat16).reshape(some, cap, LANES)
        late = imag_end.reshape(some, groups, GROUP, LANES)
        lane = lax.broadcasted_iota(jnp.int32, (some, GROUP, LANES), 2)
        packed = jnp.zeros((some, GROUP, LANES), jnp.float32)
        for g in range(groups):
            moved = pltpu.roll(late[:, g], split + g * TAIL, axis=2)
            packed = jnp.where((lane >= g * TAIL) & (lane < (g + 1) * TAIL), moved, packed)
        out_ref[at, 3 * cap :, :] = packed.astype(jnp.bfloat16)


def edge_grads(head_ids, tail_ids, neg_ids, rel, fetched):
    slots = fetched.shape[0] * ((WIRE - GROUP) // 3)
    edges = head_ids.shape[1]
    smem = pl.BlockSpec(memory_space=pltpu.SMEM)
    vmem = pl.BlockSpec(memory_space=pltpu.VMEM)
    rows = pltpu.VMEM((edges * TILES, LANES), jnp.float32)
    total = pltpu.VMEM((slots * TILES, LANES), jnp.float32)
    return pl.pallas_call(
        edge_kernel,
        in_specs=[smem, smem, smem, vmem, vmem],
        out_specs=vmem,
        out_shape=jax.ShapeDtypeStruct(fetched.shape, jnp.bfloat16),
        scratch_shapes=[
            total, rows, rows, rows, total, total, total,
            pltpu.VMEM((edges, WIDE), jnp.bfloat16),
            pltpu.VMEM((2 * edges, WIDE), jnp.bfloat16),
            pltpu.VMEM((2 * edges, edges), jnp.bfloat16),
        ],
        compiler_params=pltpu.CompilerParams(vmem_limit_bytes=VMEM_LIMIT),
        name="edges",
    )(head_ids, tail_ids, neg_ids, rel, fetched)


def local(
    entities, row_state, relations, requests, head_slots, tail_slots, neg_slots, relation_ids
):
    peer_count, slot_cap = requests.shape
    slots = peer_count * slot_cap
    wanted = lax.all_to_all(requests, "shard", split_axis=0, concat_axis=0, tiled=True)
    slab = lax.all_gather(wire_order(entities), "rep", axis=0, tiled=True)
    served = serve(wanted, slab)
    fetched = lax.all_to_all(served, "shard", split_axis=0, concat_axis=0, tiled=True)
    rel = spread(relations[relation_ids[0]].astype(jnp.float32))
    slot_grads = edge_grads(head_slots, tail_slots, neg_slots, rel, fetched)
    returned = lax.all_to_all(slot_grads, "shard", split_axis=0, concat_axis=0, tiled=True)
    slab_grads = collect(wanted.reshape(slots // LANES, LANES), returned, slab.shape[0])
    row_grads = lax.psum_scatter(slab_grads, "rep", scatter_dimension=0, tiled=True)
    row_grads = row_order(row_grads).astype(jnp.float32)
    new_state = row_state + jnp.mean(row_grads * row_grads, axis=1)
    new_entities = (
        entities.astype(jnp.float32) - learning_rate * row_grads / jnp.sqrt(new_state)[:, None]
    ).astype(jnp.bfloat16)
    return (new_entities, new_state)


def solution(mesh):
    placed = (
        P(("shard", "rep"), None),
        P(("shard", "rep")),
        P(),
        P(("shard", "rep"), None),
        P(("shard", "rep"), None),
        P(("shard", "rep"), None),
        P(("shard", "rep"), None),
        P(("shard", "rep"), None),
    )
    return jax.shard_map(
        local,
        mesh=mesh,
        in_specs=placed,
        out_specs=(P(("shard", "rep"), None), P(("shard", "rep"))),
        check_vma=False,
    )
```
